32 devices in a mesh: fsdp: 8 (over z, y), tensor: 4 (over x, core).
Axes of the slice: x: 2, y: 2, z: 4, core: 2. Of those that a mesh axis runs over, the one named last changes fastest.
Arguments:
- resid_in: bfloat16 [2048, 640], P('fsdp'), may hold values from -6 to 6
- out_cotangent: bfloat16 [2048, 640], P('fsdp'), may hold values from -6 to 6
- w_query: float32 [640, 1024], P('fsdp', 'tensor'), may hold values from -0.15811388 to 0.15811388
- w_key: float32 [640, 256], P('fsdp'), may hold values from -0.15811388 to 0.15811388
- w_value: float32 [640, 256], P('fsdp'), may hold values from -0.25 to 0.25
- w_out: float32 [1024, 640], P('tensor', 'fsdp'), may hold values from -0.1875 to 0.1875
- w_gate: float32 [640, 2048], P('fsdp', 'tensor'), may hold values from -0.25 to 0.25
- w_up: float32 [640, 2048], P('fsdp', 'tensor'), may hold values from -0.25 to 0.25
- w_down: float32 [2048, 640], P('tensor', 'fsdp'), may hold values from -0.125 to 0.125
- norm_scales: float32 [4, 640], replicated, may hold values from -0.5 to 0.5
- qk_scales: float32 [2, 256], replicated, may hold values from -0.5 to 3.4
- mom_query: float32 [640, 1024], P('fsdp', 'tensor'), may hold values from -128 to 128
- mom_key: float32 [640, 256], P('fsdp'), may hold values from -128 to 128
- mom_value: float32 [640, 256], P('fsdp'), may hold values from -128 to 128
- mom_out: float32 [1024, 640], P('tensor', 'fsdp'), may hold values from -128 to 128
- mom_gate: float32 [640, 2048], P('fsdp', 'tensor'), may hold values from -128 to 128
- mom_up: float32 [640, 2048], P('fsdp', 'tensor'), may hold values from -128 to 128
- mom_down: float32 [2048, 640], P('tensor', 'fsdp'), may hold values from -128 to 128
- mom_norms: float32 [4, 640], replicated, may hold values from -320 to 320
- mom_qk: float32 [2, 256], replicated, may hold values from -320 to 320
Outputs:
- block_out: bfloat16 [2048, 640], P('fsdp')
- resid_grad: float32 [2048, 640], P('fsdp')
- grad_query: float32 [640, 1024], P('fsdp', 'tensor')
- grad_key: float32 [640, 256], P('fsdp')
- grad_value: float32 [640, 256], P('fsdp')
- grad_out: float32 [1024, 640], P('tensor', 'fsdp')
- grad_gate: float32 [640, 2048], P('fsdp', 'tensor')
- grad_up: float32 [640, 2048], P('fsdp', 'tensor')
- grad_down: float32 [2048, 640], P('tensor', 'fsdp')
- grad_norms: float32 [4, 640], replicated
- grad_qk: float32 [2, 256], replicated
- new_query: float32 [640, 1024], P('fsdp', 'tensor')
- new_key: float32 [640, 256], P('fsdp')
- new_value: float32 [640, 256], P('fsdp')
- new_out: float32 [1024, 640], P('tensor', 'fsdp')
- new_gate: float32 [640, 2048], P('fsdp', 'tensor')
- new_up: float32 [640, 2048], P('fsdp', 'tensor')
- new_down: float32 [2048, 640], P('tensor', 'fsdp')
- new_norms: float32 [4, 640], replicated
- new_qk: float32 [2, 256], replicated
- new_mom_query: float32 [640, 1024], P('fsdp', 'tensor')
- new_mom_key: float32 [640, 256], P('fsdp')
- new_mom_value: float32 [640, 256], P('fsdp')
- new_mom_out: float32 [1024, 640], P('tensor', 'fsdp')
- new_mom_gate: float32 [640, 2048], P('fsdp', 'tensor')
- new_mom_up: float32 [640, 2048], P('fsdp', 'tensor')
- new_mom_down: float32 [2048, 640], P('tensor', 'fsdp')
- new_mom_norms: float32 [4, 640], replicated
- new_mom_qk: float32 [2, 256], replicated
The draws below stay inside these ranges and needn't reach their ends.
All inputs are finite; a program needn't handle non-finite values.
Results may differ from the reference program's by a relative error of at most 0.017.
The reference program's roundings to bfloat16 on the way count: a program that leaves them out, or rounds other values in their place, can miss the bound.
Values may be sent and summed in bfloat16 or wider, within the bound.
No kernel may reach another device: no remote copies, remote signals or barrier semaphores. Data moves between devices by JAX's collectives and lax.ppermute only.
A program may use at most 128 MiB of HBM per device.

```python
import math
import jax
import jax.numpy as jnp
from jax import lax

D = 640
HEADS = 4
HD = 256
FF = 2048
SEQ = 256
NS_STEPS = 5
FB = 512
TOKENS = 2048
N_FSDP = 8


def drawn_base(key):
    base_matrix = jax.random.truncated_normal(jax.random.fold_in(key, 101), -4.0, 4.0, (D, HEADS * HD), jnp.float32)
    noise_matrix = jax.random.truncated_normal(jax.random.fold_in(key, 102), -4.0, 4.0, (D, HD), jnp.float32)
    return (base_matrix * D ** (-0.5), noise_matrix * D ** (-0.5))


def draw_w_query(key, part):
    base_matrix, noise_matrix = drawn_base(key)
    return base_matrix


def draw_w_key(key, part):
    base_matrix, noise_matrix = drawn_base(key)
    return noise_matrix


def draw_qk_scales(key, part):
    return jax.random.uniform(jax.random.fold_in(key, 103), (2, HD), jnp.float32, -0.5, 0.5)


def strengthened(array, own_key, source, target, parts, factor):
    def block_of(position):
        return (jnp.arange(array.shape[position]) // (array.shape[position] // parts)).reshape((-1,) + (1,) * (array.ndim - 1 - position))

    first = jax.random.permutation(own_key, parts)[block_of(target)]
    other_side = (block_of(target) + parts // 2) % parts
    return jnp.where((block_of(source) == first) | (block_of(source) == other_side), factor * array, array)


def shard_levels(stream_key, shape, cuts, smallest, largest):
    loudness = 1.0
    for axis_at, parts in cuts:
        heights = jax.random.uniform(jax.random.fold_in(jax.random.fold_in(stream_key, 6), axis_at), (parts,), jnp.float32, smallest / len(cuts), largest / len(cuts))
        loudness = loudness * jnp.repeat(jnp.exp(heights), shape[axis_at] // parts).reshape((-1,) + (1,) * (len(shape) - 1 - axis_at))
    return loudness


def normal_values(stream_key, dims, width, most, cuts=(), held_as=jnp.bfloat16):
    drawn = jax.random.normal(stream_key, dims, jnp.float32) * width
    if len(cuts) > 0:
        drawn = shard_levels(stream_key, dims, cuts, -0.22, 0.18) * drawn
    return jnp.clip(drawn, min=-most, max=most).astype(held_as)


def noise_with(own_key, dims, deviation, reach, pieces, heavy, kind=jnp.bfloat16):
    values = deviation * jax.random.normal(own_key, dims, jnp.float32)
    if pieces:
        values = values * shard_levels(own_key, dims, pieces, -0.22, 0.18)
    return jnp.clip(strengthened(values, jax.random.fold_in(own_key, 3), *heavy), -reach, reach).astype(kind)


def setup_inputs(seed: int = 0) -> dict:
    splits = jax.random.split(jax.random.key(seed), 21)
    return {
        "resid_in": normal_values(splits[0], (TOKENS, D), 1.0, 6.0, ((0, 8),)),
        "out_cotangent": noise_with(splits[1], (TOKENS, D), 1.0, 6.0, ((0, 8),), (0, 1, 8, 2.0)),
        "w_query": draw_w_query(jax.random.fold_in(splits[20], 71), 0),
        "w_key": draw_w_key(jax.random.fold_in(splits[20], 71), 0),
        "w_value": normal_values(splits[4], (D, HD), D ** -0.5, 0.25, ((0, 8),), jnp.float32),
        "w_out": normal_values(splits[5], (HEADS * HD, D), (HEADS * HD) ** -0.5, 0.1875, ((0, 4), (1, 8)), jnp.float32),
        "w_gate": normal_values(splits[6], (D, FF), D ** -0.5, 0.25, ((0, 8), (1, 4)), jnp.float32),
        "w_up": normal_values(splits[7], (D, FF), D ** -0.5, 0.25, ((0, 8), (1, 4)), jnp.float32),
        "w_down": normal_values(splits[8], (FF, D), FF ** -0.5, 0.125, ((0, 4), (1, 8)), jnp.float32),
        "norm_scales": jnp.clip(jax.random.uniform(splits[9], (4, D), jnp.float32, -0.5, 0.5), -0.5, 0.5),
        "qk_scales": draw_qk_scales(jax.random.fold_in(splits[20], 71), 0),
        "mom_query": normal_values(splits[11], (D, HEADS * HD), 20.0, 128.0, ((0, 8), (1, 4)), jnp.float32),
        "mom_key": normal_values(splits[12], (D, HD), 20.0, 128.0, ((0, 8),), jnp.float32),
        "mom_value": normal_values(splits[13], (D, HD), 20.0, 128.0, ((0, 8),), jnp.float32),
        "mom_out": normal_values(splits[14], (HEADS * HD, D), 20.0, 128.0, ((0, 4), (1, 8)), jnp.float32),
        "mom_gate": normal_values(splits[15], (D, FF), 20.0, 128.0, ((0, 8), (1, 4)), jnp.float32),
        "mom_up": normal_values(splits[16], (D, FF), 20.0, 128.0, ((0, 8), (1, 4)), jnp.float32),
        "mom_down": normal_values(splits[17], (FF, D), 20.0, 128.0, ((0, 4), (1, 8)), jnp.float32),
        "mom_norms": normal_values(splits[18], (4, D), 50.0, 320.0, (), jnp.float32),
        "mom_qk": normal_values(splits[19], (2, HD), 50.0, 320.0, (), jnp.float32),
    }


EPS = 1e-06
THETA = 1000000.0
NS_A = 3.4445
NS_B = -4.775
NS_C = 2.0315
MOMENTUM = 0.95
RATE = 0.02
NEG_FILL = -1e+30

def stored(values):
    return lax.optimization_barrier(values.astype(jnp.bfloat16))

def rms_scale(values):
    return lax.rsqrt(lax.optimization_barrier(jnp.mean(values * values, axis=-1, keepdims=True)) + EPS)

def norm_backward(upstream, unit_rows, scales):
    return scales * (upstream - unit_rows * lax.optimization_barrier(jnp.mean(upstream * unit_rows, axis=-1, keepdims=True)))

def rotary_tables(length, head_width):
    half_width = head_width // 2
    exponents = jnp.arange(half_width, dtype=jnp.float32) * (-2.0 / head_width)
    frequencies = THETA ** exponents
    angles = jnp.arange(length, dtype=jnp.float32)[:, None] * frequencies[None, :]
    return (jnp.cos(angles), jnp.sin(angles))

def rotate(values, cosine_table, sine_table):
    half_width = values.shape[-1] // 2
    first_half = values[..., :half_width]
    second_half = values[..., half_width:]
    return jnp.concatenate((first_half * cosine_table - second_half * sine_table, second_half * cosine_table + first_half * sine_table), axis=-1)

def rotate_back(values, cosine_table, sine_table):
    half_width = values.shape[-1] // 2
    first_half = values[..., :half_width]
    second_half = values[..., half_width:]
    return jnp.concatenate((first_half * cosine_table + second_half * sine_table, second_half * cosine_table - first_half * sine_table), axis=-1)

def geglu(gate_pre, up_pre):
    return jax.nn.gelu(gate_pre, approximate=True) * up_pre

def orthogonalize(block_cols):
    rounded = stored(block_cols)
    widened = rounded.astype(jnp.float32)
    frobenius = jnp.sqrt(jnp.sum(widened * widened))
    current = stored(widened / (frobenius + 1e-07))
    for iteration in range(NS_STEPS):
        gram_matrix = stored(jnp.dot(current.T, current, preferred_element_type=jnp.float32))
        square = jnp.dot(gram_matrix, gram_matrix, preferred_element_type=jnp.float32)
        mixing = (NS_B * gram_matrix.astype(jnp.float32) + NS_C * square).astype(jnp.bfloat16)
        current = stored(NS_A * current.astype(jnp.float32) + jnp.dot(current, mixing, preferred_element_type=jnp.float32))
    return current.astype(jnp.float32)

def column_blocks(matrix, block_width):
    return jnp.concatenate([orthogonalize(matrix[:, offset:offset + block_width]) for offset in range(0, matrix.shape[1], block_width)], axis=1)

def one_sequence(resid_rows, cotangent_rows, weights_b, norm_scales, qk_scales, cosine_table, sine_table):
    query_w, key_w, value_w, out_w, gate_w, up_w, down_w = weights_b
    length = resid_rows.shape[0]
    head_scale = HD ** (-0.5)
    resid_f = resid_rows.astype(jnp.float32)
    scale_in = rms_scale(resid_f)
    unit_in = resid_f * scale_in
    normed_in = stored(unit_in * (1.0 + norm_scales[0]))
    query_raw = jnp.dot(normed_in, query_w, preferred_element_type=jnp.float32).reshape(length, HEADS, HD)
    key_raw = jnp.dot(normed_in, key_w, preferred_element_type=jnp.float32)
    values_b = stored(jnp.dot(normed_in, value_w, preferred_element_type=jnp.float32))
    query_scale = rms_scale(query_raw)
    query_unit = query_raw * query_scale
    query_norm = query_unit * (1.0 + qk_scales[0])
    key_scale = rms_scale(key_raw)
    key_unit = key_raw * key_scale
    key_norm = key_unit * (1.0 + qk_scales[1])
    cos_heads = cosine_table[:, None, :]
    sin_heads = sine_table[:, None, :]
    query_b = stored(rotate(query_norm, cos_heads, sin_heads) * head_scale)
    key_b = stored(rotate(key_norm, cosine_table, sine_table))
    scores = jnp.einsum('lhc,mc->hlm', query_b.astype(jnp.float32), key_b.astype(jnp.float32))
    causal = jnp.arange(length)[:, None] >= jnp.arange(length)[None, :]
    scores = jnp.where(causal[None], scores, NEG_FILL)
    row_top = lax.optimization_barrier(jnp.max(scores, axis=-1, keepdims=True))
    exp_scores = jnp.exp(scores - row_top)
    attn_probs = exp_scores / lax.optimization_barrier(jnp.sum(exp_scores, axis=-1, keepdims=True))
    probs_b = stored(attn_probs)
    attended = stored(jnp.einsum('hlm,mc->lhc', probs_b.astype(jnp.float32), values_b.astype(jnp.float32)).reshape(length, HEADS * HD))
    branch_attn = jnp.dot(attended, out_w, preferred_element_type=jnp.float32)
    scale_attn = rms_scale(branch_attn)
    unit_attn = branch_attn * scale_attn
    middle = resid_f + unit_attn * (1.0 + norm_scales[1])
    scale_ffn = rms_scale(middle)
    unit_ffn = middle * scale_ffn
    normed_ffn = stored(unit_ffn * (1.0 + norm_scales[2]))
    gate_pre = jnp.dot(normed_ffn, gate_w, preferred_element_type=jnp.float32)
    up_pre = jnp.dot(normed_ffn, up_w, preferred_element_type=jnp.float32)
    hidden = stored(geglu(gate_pre, up_pre))
    branch_ffn = jnp.dot(hidden, down_w, preferred_element_type=jnp.float32)
    scale_out = rms_scale(branch_ffn)
    unit_out = branch_ffn * scale_out
    block_out = (middle + unit_out * (1.0 + norm_scales[3])).astype(jnp.bfloat16)
    d_out = cotangent_rows.astype(jnp.float32)
    grad_out_scale = lax.optimization_barrier(jnp.sum(d_out * unit_out, axis=0))
    d_ffn = stored(norm_backward(d_out * (1.0 + norm_scales[3]), unit_out, scale_out))
    grad_down = jnp.dot(hidden.T, d_ffn, preferred_element_type=jnp.float32)
    d_hidden = jnp.dot(d_ffn, down_w.T, preferred_element_type=jnp.float32)
    pullback = jax.vjp(geglu, gate_pre, up_pre)[1]
    d_gate_f, d_up_f = pullback(d_hidden)
    d_gate = stored(d_gate_f)
    d_up = stored(d_up_f)
    grad_gate = jnp.dot(normed_ffn.T, d_gate, preferred_element_type=jnp.float32)
    grad_up = jnp.dot(normed_ffn.T, d_up, preferred_element_type=jnp.float32)
    d_normed_ffn = jnp.dot(d_gate, gate_w.T, preferred_element_type=jnp.float32) + jnp.dot(d_up, up_w.T, preferred_element_type=jnp.float32)
    grad_ffn_in = lax.optimization_barrier(jnp.sum(d_normed_ffn * unit_ffn, axis=0))
    d_middle = d_out + norm_backward(d_normed_ffn * (1.0 + norm_scales[2]), unit_ffn, scale_ffn)
    grad_attn_out = lax.optimization_barrier(jnp.sum(d_middle * unit_attn, axis=0))
    d_attn = stored(norm_backward(d_middle * (1.0 + norm_scales[1]), unit_attn, scale_attn))
    grad_out = jnp.dot(attended.T, d_attn, preferred_element_type=jnp.float32)
    d_attended = stored(jnp.dot(d_attn, out_w.T, preferred_element_type=jnp.float32)).reshape(length, HEADS, HD)
    d_probs = jnp.einsum('lhc,mc->hlm', d_attended.astype(jnp.float32), values_b.astype(jnp.float32))
    d_scores = stored(attn_probs * (d_probs - lax.optimization_barrier(jnp.sum(attn_probs * d_probs, axis=-1, keepdims=True))))
    d_query_rot = head_scale * jnp.einsum('hlm,mc->lhc', d_scores.astype(jnp.float32), key_b.astype(jnp.float32))
    d_key_rot = jnp.einsum('hlm,lhc->hmc', d_scores.astype(jnp.float32), query_b.astype(jnp.float32))
    d_values = stored(jnp.einsum('hlm,lhc->hmc', probs_b.astype(jnp.float32), d_attended.astype(jnp.float32)))
    d_query_norm = rotate_back(d_query_rot, cos_heads, sin_heads)
    d_key_norm = rotate_back(d_key_rot, cosine_table[None], sine_table[None])
    grad_query_scale = lax.optimization_barrier(jnp.sum(d_query_norm * query_unit, axis=(0, 1)))
    grad_key_scale = lax.optimization_barrier(jnp.sum(d_key_norm * key_unit[None], axis=(0, 1)))
    d_query = stored(norm_backward(d_query_norm * (1.0 + qk_scales[0]), query_unit, query_scale)).reshape(length, HEADS * HD)
    d_key = stored(norm_backward(d_key_norm * (1.0 + qk_scales[1]), key_unit[None], key_scale[None]))
    grad_query = jnp.dot(normed_in.T, d_query, preferred_element_type=jnp.float32)
    grad_key = jnp.einsum('ld,hlc->dc', normed_in.astype(jnp.float32), d_key.astype(jnp.float32))
    grad_value = jnp.einsum('ld,hlc->dc', normed_in.astype(jnp.float32), d_values.astype(jnp.float32))
    d_normed_in = jnp.dot(d_query, query_w.T, preferred_element_type=jnp.float32)
    d_normed_in = d_normed_in + jnp.einsum('hlc,dc->ld', d_key.astype(jnp.float32), key_w.astype(jnp.float32))
    d_normed_in = d_normed_in + jnp.einsum('hlc,dc->ld', d_values.astype(jnp.float32), value_w.astype(jnp.float32))
    grad_in_scale = lax.optimization_barrier(jnp.sum(d_normed_in * unit_in, axis=0))
    resid_grad = d_middle + norm_backward(d_normed_in * (1.0 + norm_scales[0]), unit_in, scale_in)
    gradients = (grad_query, grad_key, grad_value, grad_out, grad_gate, grad_up, grad_down, jnp.stack((grad_in_scale, grad_attn_out, grad_ffn_in, grad_out_scale)), jnp.stack((grad_query_scale, grad_key_scale)))
    return ((block_out, resid_grad), gradients)

def reference(resid_in, out_cotangent, w_query, w_key, w_value, w_out, w_gate, w_up, w_down, norm_scales, qk_scales, mom_query, mom_key, mom_value, mom_out, mom_gate, mom_up, mom_down, mom_norms, mom_qk):
    weights = (w_query, w_key, w_value, w_out, w_gate, w_up, w_down)
    weights_b = tuple((stored(weight) for weight in weights))
    cosine_table, sine_table = rotary_tables(SEQ, HD)

    def per_sequence(totals, rows_pair):
        outputs, gradients = one_sequence(rows_pair[0], rows_pair[1], weights_b, norm_scales, qk_scales, cosine_table, sine_table)
        return (jax.tree.map(jnp.add, totals, gradients), outputs)
    initial = tuple((jnp.zeros_like(weight) for weight in weights)) + (jnp.zeros_like(norm_scales), jnp.zeros_like(qk_scales))
    gradients, outputs = lax.scan(per_sequence, initial, (resid_in.reshape(N_FSDP, SEQ, D), out_cotangent.reshape(N_FSDP, SEQ, D)))
    block_out = outputs[0].reshape(TOKENS, D)
    resid_grad = outputs[1].reshape(TOKENS, D)
    moments = (mom_query, mom_key, mom_value, mom_out, mom_gate, mom_up, mom_down)
    new_moms = tuple((MOMENTUM * moment + gradient for moment, gradient in zip(moments, gradients[:7])))
    step_size = RATE * 0.2 * math.sqrt(D)
    orthos = (column_blocks(new_moms[0], HD), column_blocks(new_moms[1], HD), column_blocks(new_moms[2], HD), column_blocks(new_moms[3].T, HD).T, column_blocks(new_moms[4], FB), column_blocks(new_moms[5], FB), column_blocks(new_moms[6].T, FB).T)
    new_weights = tuple((weight - step_size * ortho_block for weight, ortho_block in zip(weights, orthos)))
    new_mom_norms = MOMENTUM * mom_norms + gradients[7]
    new_mom_qk = MOMENTUM * mom_qk + gradients[8]
    gain_rate = 0.2 / math.sqrt(TOKENS)
    new_norms = norm_scales - gain_rate * new_mom_norms
    new_qk = qk_scales - gain_rate * new_mom_qk
    return (block_out, resid_grad, gradients[0], gradients[1], gradients[2], gradients[3], gradients[4], gradients[5], gradients[6], gradients[7], gradients[8], new_weights[0], new_weights[1], new_weights[2], new_weights[3], new_weights[4], new_weights[5], new_weights[6], new_norms, new_qk, new_moms[0], new_moms[1], new_moms[2], new_moms[3], new_moms[4], new_moms[5], new_moms[6], new_mom_norms, new_mom_qk)
```

```python
import math

import jax
import jax.numpy as jnp
from jax import lax
from jax.experimental import pallas as pl
from jax.experimental.pallas import tpu as pltpu
from jax.sharding import PartitionSpec as P

NS_STEPS = 5


EPS = 1e-06
THETA = 1000000.0
NS_A = 3.4445
NS_B = -4.775
NS_C = 2.0315
MOMENTUM = 0.95
RATE = 0.02
NEG_FILL = -1e30


def rms_scale(values):
    return lax.rsqrt(jnp.mean(values * values, axis=-1, keepdims=True) + EPS)


def norm_backward(upstream, unit_rows, scales):
    return scales * (upstream - unit_rows * jnp.mean(upstream * unit_rows, axis=-1, keepdims=True))


def rotary_tables(length, head_width):
    half_width = head_width // 2
    exponents = jnp.arange(half_width, dtype=jnp.float32) * (-2.0 / head_width)
    frequencies = THETA**exponents
    angles = jnp.arange(length, dtype=jnp.float32)[:, None] * frequencies[None, :]
    return (jnp.cos(angles), jnp.sin(angles))


def rotate(values, cosine_table, sine_table):
    half_width = values.shape[-1] // 2
    first_half = values[..., :half_width]
    second_half = values[..., half_width:]
    return jnp.concatenate(
        (
            first_half * cosine_table - second_half * sine_table,
            second_half * cosine_table + first_half * sine_table,
        ),
        axis=-1,
    )


def rotate_back(values, cosine_table, sine_table):
    half_width = values.shape[-1] // 2
    first_half = values[..., :half_width]
    second_half = values[..., half_width:]
    return jnp.concatenate(
        (
            first_half * cosine_table + second_half * sine_table,
            second_half * cosine_table - first_half * sine_table,
        ),
        axis=-1,
    )


def geglu(gate_pre, up_pre):
    return jax.nn.gelu(gate_pre, approximate=True) * up_pre


def orthogonalize(block_b):
    widened = block_b.astype(jnp.float32)
    frobenius = jnp.sqrt(jnp.sum(widened * widened))
    current = lax.optimization_barrier((widened / (frobenius + 1e-07)).astype(jnp.bfloat16))
    for iteration in range(NS_STEPS):
        gram_matrix = lax.optimization_barrier(
            jnp.einsum("dr,ds->rs", current, current, preferred_element_type=jnp.float32).astype(
                jnp.bfloat16
            )
        )
        square = jnp.dot(gram_matrix, gram_matrix, preferred_element_type=jnp.float32)
        mixing = (NS_B * gram_matrix.astype(jnp.float32) + NS_C * square).astype(jnp.bfloat16)
        current = lax.optimization_barrier(
            (
                NS_A * current.astype(jnp.float32)
                + jnp.dot(current, mixing, preferred_element_type=jnp.float32)
            ).astype(jnp.bfloat16)
        )
    return current


def exchange(values, axis, distance):
    count = lax.axis_size(axis)
    return lax.ppermute(values, axis, [(rank, rank ^ distance) for rank in range(count)])


def stages(count):
    found = []
    stride = 1
    while stride < count:
        size = 2 if stride == 1 else min(4, count // stride)
        found.append((stride, size))
        stride *= size
    return found


def place_kernel(rank_ref, *refs):
    whole_ref = refs[-1]
    for distance, piece_ref in enumerate(refs[:-1]):
        whole_ref[rank_ref[0] ^ distance] = piece_ref[...]


def place_pieces(rank, pieces):
    rows, columns = pieces[0].shape
    count = len(pieces)
    whole = pl.pallas_call(
        place_kernel,
        out_shape=jax.ShapeDtypeStruct((count, rows, columns), pieces[0].dtype),
        in_specs=[pl.BlockSpec(memory_space=pltpu.SMEM)]
        + [pl.BlockSpec(memory_space=pltpu.VMEM)] * count,
        out_specs=pl.BlockSpec(memory_space=pltpu.VMEM),
        name="place_pieces",
    )(rank.reshape(1).astype(jnp.int32), *pieces)
    return whole.reshape(count * rows, columns)


def gather_rows(shard, axis):
    pieces = {0: shard}
    for stride, size in reversed(stages(lax.axis_size(axis))):
        grown = {}
        for distance, piece in pieces.items():
            for step in range(size):
                moved = piece if step == 0 else exchange(piece, axis, step * stride)
                grown[distance ^ (step * stride)] = moved
        pieces = grown
    return place_pieces(lax.axis_index(axis), [pieces[place] for place in range(len(pieces))])


def reduce_rows(total, axis):
    count = lax.axis_size(axis)
    rank = lax.axis_index(axis)
    current = total.reshape(count, total.shape[0] // count, total.shape[1])
    for stride, size in stages(count):
        digit = (rank // stride) % size
        grouped = current.reshape((current.shape[0] // size, size) + current.shape[1:])
        arrived = [
            exchange(
                lax.dynamic_index_in_dim(grouped, digit ^ step, 1, False).astype(jnp.bfloat16),
                axis,
                step * stride,
            )
            for step in range(1, size)
        ]
        current = lax.dynamic_index_in_dim(grouped, digit, 1, False)
        for piece in arrived:
            current = current + piece.astype(jnp.float32)
    return current[0]


def on_device(
    resid_in,
    out_cotangent,
    w_query,
    w_key,
    w_value,
    w_out,
    w_gate,
    w_up,
    w_down,
    norm_scales,
    qk_scales,
    mom_query,
    mom_key,
    mom_value,
    mom_out,
    mom_gate,
    mom_up,
    mom_down,
    mom_norms,
    mom_qk,
):
    fsdp_rank = lax.axis_index("fsdp")
    tensor_rank = lax.axis_index("tensor")
    fsdp_count = lax.axis_size("fsdp")
    tensor_count = lax.axis_size("tensor")
    length = resid_in.shape[0]
    model_width = resid_in.shape[1]
    head_width = w_query.shape[1]
    hidden_width = w_gate.shape[1]
    head_scale = head_width ** (-0.5)
    side = tensor_rank % 2
    half = length // 2

    qkv_weight = gather_rows(
        jnp.concatenate((w_query, w_key, w_value), axis=1).astype(jnp.bfloat16), "fsdp"
    )
    out_weight_t = gather_rows(w_out.T.astype(jnp.bfloat16), "fsdp")
    gate_up_weight = gather_rows(
        jnp.concatenate((w_gate, w_up), axis=1).astype(jnp.bfloat16), "fsdp"
    )
    down_weight_t = gather_rows(w_down.T.astype(jnp.bfloat16), "fsdp")

    def own_half(values):
        return lax.dynamic_slice_in_dim(values, side * half, half, 0)

    def half_total(partial_value):
        total = own_half(partial_value) + exchange(
            lax.dynamic_slice_in_dim(partial_value, (1 - side) * half, half, 0), "tensor", 1
        )
        distance = 2
        while distance < tensor_count:
            rounded = lax.optimization_barrier(total.astype(jnp.bfloat16))
            total = rounded.astype(jnp.float32) + exchange(rounded, "tensor", distance).astype(
                jnp.float32
            )
            distance *= 2
        return total

    def both_halves(values):
        other = exchange(values, "tensor", 1)
        return jnp.where(
            side == 0,
            jnp.concatenate((values, other), axis=0),
            jnp.concatenate((other, values), axis=0),
        )

    replicas = tensor_count // 2
    share = half // replicas
    share_start = (tensor_rank // 2) * share

    def rows_sum(left, right):
        return jnp.sum(
            lax.dynamic_slice_in_dim(left, share_start, share, 0)
            * lax.dynamic_slice_in_dim(right, share_start, share, 0),
            axis=0,
        )

    cosine_table, sine_table = rotary_tables(length, head_width)
    resid_f = resid_in.astype(jnp.float32)
    scale_in = rms_scale(resid_f)
    unit_in = resid_f * scale_in
    normed_in = (unit_in * (1.0 + norm_scales[0])).astype(jnp.bfloat16)
    projected = jnp.dot(normed_in, qkv_weight, preferred_element_type=jnp.float32)
    query_raw = projected[:, :head_width]
    key_raw = projected[:, head_width : 2 * head_width]
    values_b = projected[:, 2 * head_width :].astype(jnp.bfloat16)
    query_scale = rms_scale(query_raw)
    query_unit = query_raw * query_scale
    query_norm = query_unit * (1.0 + qk_scales[0])
    key_scale = rms_scale(key_raw)
    key_unit = key_raw * key_scale
    key_norm = key_unit * (1.0 + qk_scales[1])
    query_b = (rotate(query_norm, cosine_table, sine_table) * head_scale).astype(jnp.bfloat16)
    key_b = rotate(key_norm, cosine_table, sine_table).astype(jnp.bfloat16)
    scores = jnp.einsum("qc,kc->qk", query_b, key_b, preferred_element_type=jnp.float32)
    positions = jnp.arange(length, dtype=jnp.int32)
    scores = jnp.where(positions[None, :] <= positions[:, None], scores, NEG_FILL)
    exp_scores = jnp.exp(scores - jnp.max(scores, axis=-1, keepdims=True))
    attn_probs = exp_scores / jnp.sum(exp_scores, axis=-1, keepdims=True)
    probs_b = attn_probs.astype(jnp.bfloat16)
    attended = jnp.dot(probs_b, values_b, preferred_element_type=jnp.float32).astype(jnp.bfloat16)
    branch_attn = half_total(
        jnp.einsum("lc,dc->ld", attended, out_weight_t, preferred_element_type=jnp.float32)
    )

    resid_h = own_half(resid_f)
    d_out = own_half(out_cotangent).astype(jnp.float32)
    scale_attn = rms_scale(branch_attn)
    unit_attn = branch_attn * scale_attn
    middle = resid_h + unit_attn * (1.0 + norm_scales[1])
    scale_ffn = rms_scale(middle)
    unit_ffn = middle * scale_ffn
    normed_ffn = both_halves((unit_ffn * (1.0 + norm_scales[2])).astype(jnp.bfloat16))
    hidden_pair = jnp.dot(normed_ffn, gate_up_weight, preferred_element_type=jnp.float32)
    gate_pre = hidden_pair[:, :hidden_width]
    up_pre = hidden_pair[:, hidden_width:]
    hidden = geglu(gate_pre, up_pre).astype(jnp.bfloat16)
    branch_ffn = half_total(
        jnp.einsum("lf,df->ld", hidden, down_weight_t, preferred_element_type=jnp.float32)
    )
    scale_out = rms_scale(branch_ffn)
    unit_out = branch_ffn * scale_out
    d_ffn = both_halves(
        norm_backward(d_out * (1.0 + norm_scales[3]), unit_out, scale_out).astype(jnp.bfloat16)
    )
    block_out = both_halves((middle + unit_out * (1.0 + norm_scales[3])).astype(jnp.bfloat16))
    grad_out_scale = rows_sum(d_out, unit_out)

    d_hidden = jnp.dot(d_ffn, down_weight_t, preferred_element_type=jnp.float32)
    d_gate_f, d_up_f = jax.vjp(geglu, gate_pre, up_pre)[1](d_hidden)
    d_pair = jnp.concatenate((d_gate_f, d_up_f), axis=1).astype(jnp.bfloat16)
    d_normed_ffn = half_total(
        jnp.einsum("lf,df->ld", d_pair, gate_up_weight, preferred_element_type=jnp.float32)
    )
    grad_down_t = jnp.einsum("ld,lf->df", d_ffn, hidden, preferred_element_type=jnp.float32)
    shard_down_t = reduce_rows(grad_down_t, "fsdp")
    grad_pair = jnp.einsum("ld,lf->df", normed_ffn, d_pair, preferred_element_type=jnp.float32)
    shard_pair = reduce_rows(grad_pair, "fsdp")

    grad_ffn_in = rows_sum(d_normed_ffn, unit_ffn)
    d_middle = d_out + norm_backward(d_normed_ffn * (1.0 + norm_scales[2]), unit_ffn, scale_ffn)
    grad_attn_out = rows_sum(d_middle, unit_attn)
    d_attn = both_halves(
        norm_backward(d_middle * (1.0 + norm_scales[1]), unit_attn, scale_attn).astype(jnp.bfloat16)
    )
    grad_out_t = jnp.einsum("ld,lc->dc", d_attn, attended, preferred_element_type=jnp.float32)
    shard_out_t = reduce_rows(grad_out_t, "fsdp")
    d_attended = jnp.dot(d_attn, out_weight_t, preferred_element_type=jnp.float32).astype(
        jnp.bfloat16
    )
    d_probs = jnp.einsum("qc,kc->qk", d_attended, values_b, preferred_element_type=jnp.float32)
    d_scores = (
        attn_probs * (d_probs - jnp.sum(attn_probs * d_probs, axis=-1, keepdims=True))
    ).astype(jnp.bfloat16)
    d_query_rot = head_scale * jnp.dot(d_scores, key_b, preferred_element_type=jnp.float32)
    d_key_rot = jnp.einsum("qk,qc->kc", d_scores, query_b, preferred_element_type=jnp.float32)
    d_values = jnp.einsum("qk,qc->kc", probs_b, d_attended, preferred_element_type=jnp.float32)
    d_query_norm = rotate_back(d_query_rot, cosine_table, sine_table)
    d_key_norm = rotate_back(d_key_rot, cosine_table, sine_table)
    grad_query_scale = jnp.sum(d_query_norm * query_unit, axis=0)
    grad_key_scale = jnp.sum(d_key_norm * key_unit, axis=0)
    d_query = norm_backward(
        d_query_norm * (1.0 + qk_scales[0]), query_unit, query_scale
    ).astype(jnp.bfloat16)
    d_key = norm_backward(d_key_norm * (1.0 + qk_scales[1]), key_unit, key_scale)
    d_key_value = jnp.concatenate((d_key, d_values), axis=1).astype(jnp.bfloat16)

    columns_start = jnp.int32(0)
    distance = 1
    while distance < tensor_count:
        bit = (tensor_rank // distance) % 2
        width = d_key_value.shape[1] // 2
        sent = lax.dynamic_slice_in_dim(d_key_value, (1 - bit) * width, width, 1)
        kept = lax.dynamic_slice_in_dim(d_key_value, bit * width, width, 1)
        arrived = exchange(sent.astype(jnp.bfloat16), "tensor", distance)
        d_key_value = kept.astype(jnp.float32) + arrived.astype(jnp.float32)
        columns_start = columns_start + bit * width
        distance *= 2
    d_proj = jnp.concatenate((d_query, d_key_value.astype(jnp.bfloat16)), axis=1)
    own_width = d_key_value.shape[1]
    own_weight = jnp.concatenate(
        (
            qkv_weight[:, :head_width],
            lax.dynamic_slice_in_dim(qkv_weight, head_width + columns_start, own_width, 1),
        ),
        axis=1,
    )
    grad_proj = jnp.einsum("ld,lc->dc", normed_in, d_proj, preferred_element_type=jnp.float32)
    shard_proj = reduce_rows(grad_proj, "fsdp")
    shard_query = shard_proj[:, :head_width]
    shard_key_value = shard_proj[:, head_width:]
    distance = tensor_count // 2
    while distance >= 1:
        bit = (tensor_rank // distance) % 2
        other = exchange(shard_key_value, "tensor", distance)
        shard_key_value = jnp.where(
            bit == 0,
            jnp.concatenate((shard_key_value, other), axis=1),
            jnp.concatenate((other, shard_key_value), axis=1),
        )
        distance //= 2
    d_normed_in = half_total(
        jnp.einsum("lc,dc->ld", d_proj, own_weight, preferred_element_type=jnp.float32)
    )
    unit_in_h = own_half(unit_in)
    grad_in_scale = rows_sum(d_normed_in, unit_in_h)
    resid_grad = both_halves(
        d_middle
        + norm_backward(d_normed_in * (1.0 + norm_scales[0]), unit_in_h, own_half(scale_in))
    )

    small = jnp.concatenate(
        (
            jnp.concatenate((grad_in_scale, grad_attn_out, grad_ffn_in, grad_out_scale)),
            jnp.concatenate((grad_query_scale, grad_key_scale)),
        )
    )
    for axis in ("tensor", "fsdp"):
        distance = 1
        while distance < lax.axis_size(axis):
            small = small + exchange(small, axis, distance)
            distance *= 2
    grad_norms = small[: 4 * model_width].reshape(4, model_width)
    grad_qk = small[4 * model_width :].reshape(2, head_width)

    shard_grads = (
        shard_query,
        shard_key_value[:, :head_width],
        shard_key_value[:, head_width:],
        shard_out_t.T,
        shard_pair[:, :hidden_width],
        shard_pair[:, hidden_width:],
        shard_down_t.T,
    )
    moments = (mom_query, mom_key, mom_value, mom_out, mom_gate, mom_up, mom_down)
    new_moms = tuple(
        (MOMENTUM * moment + gradient for moment, gradient in zip(moments, shard_grads))
    )
    col_forms = (
        new_moms[0],
        new_moms[1],
        new_moms[2],
        new_moms[3].T,
        new_moms[4],
        new_moms[5],
        new_moms[6].T,
    )
    widths = [column.shape[1] for column in col_forms]
    widest = max(widths)
    stride = fsdp_count // 7
    owners = [member * stride for member in range(7)]
    rows = col_forms[0].shape[0]
    packs = [jnp.zeros((rows, widest), jnp.bfloat16)] * fsdp_count
    for member in range(7):
        packs[owners[member]] = jnp.pad(
            col_forms[member].astype(jnp.bfloat16), ((0, 0), (0, widest - widths[member]))
        )
    owned = lax.all_to_all(jnp.concatenate(packs, axis=0), "fsdp", 0, 0, tiled=True)
    pieces = lax.all_to_all(orthogonalize(owned), "fsdp", 0, 0, tiled=True)
    pieces = [
        pieces[owners[member] * rows : (owners[member] + 1) * rows, : widths[member]].astype(
            jnp.float32
        )
        for member in range(7)
    ]
    step_size = RATE * 0.2 * math.sqrt(model_width)
    updates = (pieces[0], pieces[1], pieces[2], pieces[3].T, pieces[4], pieces[5], pieces[6].T)
    weights = (w_query, w_key, w_value, w_out, w_gate, w_up, w_down)
    new_weights = tuple((weight - step_size * update for weight, update in zip(weights, updates)))
    new_mom_norms = MOMENTUM * mom_norms + grad_norms
    new_mom_qk = MOMENTUM * mom_qk + grad_qk
    gain_rate = 0.2 / math.sqrt(length * fsdp_count)
    new_norms = norm_scales - gain_rate * new_mom_norms
    new_qk = qk_scales - gain_rate * new_mom_qk
    return (
        (block_out, resid_grad)
        + shard_grads
        + (grad_norms, grad_qk)
        + new_weights
        + (new_norms, new_qk)
        + new_moms
        + (new_mom_norms, new_mom_qk)
    )


def solution(mesh):
    return jax.shard_map(
        on_device,
        mesh=mesh,
        in_specs=(
            P("fsdp", None),
            P("fsdp", None),
            P("fsdp", "tensor"),
            P("fsdp", None),
            P("fsdp", None),
            P("tensor", "fsdp"),
            P("fsdp", "tensor"),
            P("fsdp", "tensor"),
            P("tensor", "fsdp"),
            P(),
            P(),
            P("fsdp", "tensor"),
            P("fsdp", None),
            P("fsdp", None),
            P("tensor", "fsdp"),
            P("fsdp", "tensor"),
            P("fsdp", "tensor"),
            P("tensor", "fsdp"),
            P(),
            P(),
        ),
        out_specs=(
            P("fsdp", None),
            P("fsdp", None),
            P("fsdp", "tensor"),
            P("fsdp", None),
            P("fsdp", None),
            P("tensor", "fsdp"),
            P("fsdp", "tensor"),
            P("fsdp", "tensor"),
            P("tensor", "fsdp"),
            P(),
            P(),
            P("fsdp", "tensor"),
            P("fsdp", None),
            P("fsdp", None),
            P("tensor", "fsdp"),
            P("fsdp", "tensor"),
            P("fsdp", "tensor"),
            P("tensor", "fsdp"),
            P(),
            P(),
            P("fsdp", "tensor"),
            P("fsdp", None),
            P("fsdp", None),
            P("tensor", "fsdp"),
            P("fsdp", "tensor"),
            P("fsdp", "tensor"),
            P("tensor", "fsdp"),
            P(),
            P(),
        ),
        check_vma=False,
    )
```
